512 devices in a mesh: dp: 16 (over z, core), mp: 32 (over y, x).
Axes of the slice: x: 4, y: 8, z: 8, core: 2. Of those that a mesh axis runs over, the one named last changes fastest.
Arguments:
- activations: bfloat16 [32768, 8192], P('dp', 'mp'), as said below
- output_grads: bfloat16 [32768, 28672], P('dp', 'mp'), as said below
- probe_matrix: bfloat16 [28672, 128], P('mp'), may hold values from -6 to 6
Outputs:
- basis: float32 [8192, 128], P('mp')
- projection: float32 [128, 28672], P(None, 'mp')
The draws below stay inside these ranges and needn't reach their ends.
Inputs may be any that keep to these rules, and one draw needn't show every extreme that they name: `activations`: finite real values of order one. `output_grads`: finite real values of order one.
All inputs are finite; a program needn't handle non-finite values.
Results may differ from the reference program's by a relative error of at most 0.035.
Values may be sent and summed in bfloat16 or wider, within the bound.
No kernel may reach another device: no remote copies, remote signals or barrier semaphores. Data moves between devices by JAX's collectives and lax.ppermute only.
A program may use at most 64 MiB of HBM per device.

```python
import jax
import jax.numpy as jnp
from jax import lax

H = 8192
F = 28672
K = 128
TOKENS = 32768
N_MP = 32


def column_scales(key, width, blocks, spread):
    position = jnp.arange(width, dtype=jnp.float32)
    span = width // blocks
    inner = (jnp.arange(width) % span).astype(jnp.float32) / span
    rough = jax.random.uniform(key, (width,), jnp.float32, 0.7, 1.4)
    return jnp.exp(jnp.log(spread) * (position + 0.5) / width + jnp.log(3.0) * inner) * rough


def scaled_field(key, rows, width, blocks):
    first_key, second_key = jax.random.split(key, 2)
    spread = 30.0
    noise = jnp.clip(jax.random.normal(first_key, (rows, width), jnp.float32), -6.0, 6.0)
    scales = column_scales(second_key, width, blocks, spread)
    scales = scales / jnp.sqrt(jnp.mean(scales * scales))
    return noise * scales


def draw_activations(key, part):
    field = scaled_field(jax.random.fold_in(key, 11), TOKENS, H, N_MP)
    return (field / jnp.sqrt(jnp.float32(TOKENS))).astype(jnp.bfloat16)


def draw_output_grads(key, part):
    field = scaled_field(jax.random.fold_in(key, 23), TOKENS, F, N_MP)
    return field.astype(jnp.bfloat16)


def shard_levels(rng, dims, shards, least, high):
    factor_of, own = 1.0, jax.random.fold_in(rng, 6)
    for dim, blocks in shards:
        heights = jnp.exp(jax.random.uniform(jax.random.fold_in(own, dim), (blocks,), jnp.float32, least / len(shards), high / len(shards)))
        factor_of = factor_of * jnp.repeat(heights, dims[dim] // blocks).reshape([-1 if axis == dim else 1 for axis in range(len(dims))])
    return factor_of


def scatter_about(key, dims, deviation, most, cuts=(), held_as=jnp.bfloat16):
    values = jax.random.normal(key, dims, jnp.float32) * deviation
    if len(cuts) > 0:
        values = shard_levels(key, dims, cuts, -0.22, 0.18) * values
    return jnp.clip(values, min=-most, max=most).astype(held_as)


def setup_inputs(seed: int = 0) -> dict:
    seeds = jax.random.split(jax.random.key(seed), 4)
    activations = draw_activations(jax.random.fold_in(seeds[3], 71), 0)
    output_grads = draw_output_grads(jax.random.fold_in(seeds[3], 71), 0)
    probe_matrix = scatter_about(seeds[2], (F, K), 1.0, 6.0, ((0, 32),))
    return {"activations": activations, "output_grads": output_grads, "probe_matrix": probe_matrix}


def contract_rows(left, right):
    return lax.dot_general(left.astype(jnp.float32), right.astype(jnp.float32), (((0,), (0,)), ((), ())), preferred_element_type=jnp.float32)

def blocked_total(left, right):
    span = left.shape[1] // N_MP

    def add_block(index, total):
        start = (index * span).astype(jnp.int32)
        columns = lax.dynamic_slice_in_dim(left, start, span, 1)
        pieces = lax.dynamic_slice_in_dim(right, start, span, 0)
        term = jnp.dot(columns.astype(jnp.float32), pieces.astype(jnp.float32), preferred_element_type=jnp.float32)
        term = lax.optimization_barrier(term.astype(jnp.bfloat16)).astype(jnp.float32)
        return total + term
    start_total = jnp.zeros((left.shape[0], right.shape[1]), jnp.float32)
    return lax.fori_loop(0, N_MP, add_block, start_total).astype(jnp.bfloat16)

def orthonormalize(matrix):
    gram_matrix = lax.dot_general(matrix.astype(jnp.float32), matrix.astype(jnp.float32), (((0,), (0,)), ((), ())), precision=lax.Precision.HIGHEST, preferred_element_type=jnp.float32)
    factor = jnp.linalg.cholesky(gram_matrix)
    return lax.linalg.triangular_solve(factor, matrix, left_side=False, lower=True, transpose_a=True)

def reference(activations, output_grads, probe_matrix):
    probe_rows = blocked_total(output_grads, probe_matrix)
    first_basis = orthonormalize(contract_rows(activations, probe_rows))
    token_rows = blocked_total(activations, first_basis.astype(jnp.bfloat16))
    second_basis = orthonormalize(contract_rows(output_grads, token_rows))
    unit_rows = blocked_total(output_grads, second_basis.astype(jnp.bfloat16))
    third_basis = orthonormalize(contract_rows(activations, unit_rows))
    last_rows = blocked_total(activations, third_basis.astype(jnp.bfloat16))
    projection = contract_rows(last_rows, output_grads)
    basis = third_basis * jnp.sqrt(jnp.float32(H))
    return (basis, projection)
```

```python
import jax
import jax.numpy as jnp
from jax import lax
from jax.sharding import PartitionSpec as P

H = 8192
N_MP = 32
N_DP = 16
K = 128
HIGHEST = lax.Precision.HIGHEST


def rows_product(left, right):
    return lax.dot_general(
        left, right, (((0,), (0,)), ((), ())), preferred_element_type=jnp.float32
    )


def split_two(matrix):
    high = matrix.astype(jnp.bfloat16)
    low = (matrix - high.astype(jnp.float32)).astype(jnp.bfloat16)
    return jnp.concatenate([high, low], axis=1)


def exchange(blocks, axis):
    return lax.all_to_all(blocks, axis, 0, 0)


def scatter_sum(blocks, axis):
    return jnp.sum(exchange(blocks, axis).astype(jnp.float32), axis=0)


def gather(block, axis, count):
    return exchange(jnp.broadcast_to(block[None], (count,) + block.shape), axis)


def sum_over_tokens(partial_value):
    rows, columns = partial_value.shape
    mine = scatter_sum(partial_value.reshape(N_DP, rows // N_DP, columns), "dp")
    return gather(mine, "dp", N_DP).reshape(rows, columns)


def token_rows_of(data, sketch):
    tokens = data.shape[0]
    gram = lax.dot_general(
        sketch, sketch, (((0,), (0,)), ((), ())), precision=HIGHEST,
        preferred_element_type=jnp.float32,
    )
    both = jnp.dot(data, split_two(sketch), preferred_element_type=jnp.float32)
    product = both[:, :K] + both[:, K:]
    span = tokens // N_MP
    blocks = jnp.concatenate(
        [product.reshape(N_MP, span, K), gram.reshape(N_MP, K // N_MP, K),
         jnp.zeros((N_MP, K // N_MP, K), jnp.float32)], axis=1
    )
    whole = gather(scatter_sum(blocks, "mp"), "mp", N_MP)
    gram = whole[:, span:span + K // N_MP].reshape(K, K)
    factor = jnp.linalg.cholesky(gram)
    inverse = lax.linalg.triangular_solve(
        factor, jnp.eye(K, dtype=jnp.float32), left_side=False, lower=True, transpose_a=True
    )
    product = whole[:, :span].reshape(tokens, K)
    rows = jnp.dot(product, inverse, precision=HIGHEST, preferred_element_type=jnp.float32)
    return rows.astype(jnp.bfloat16), inverse


def on_device(activations, output_grads, probe_matrix):
    tokens = activations.shape[0]
    partial_value = jnp.dot(output_grads, probe_matrix, preferred_element_type=jnp.float32)
    mine = scatter_sum(partial_value.astype(jnp.bfloat16).reshape(N_MP, tokens // N_MP, K), "mp")
    probe_rows = gather(mine.astype(jnp.bfloat16), "mp", N_MP).reshape(tokens, K)

    sketch = sum_over_tokens(rows_product(activations, probe_rows))
    token_rows, _ = token_rows_of(activations, sketch)
    back_sketch = sum_over_tokens(rows_product(output_grads, token_rows))
    unit_rows, _ = token_rows_of(output_grads, back_sketch)
    power_sketch = sum_over_tokens(rows_product(activations, unit_rows))
    last_rows, inverse = token_rows_of(activations, power_sketch)
    projection = sum_over_tokens(rows_product(last_rows, output_grads))
    third_basis = jnp.dot(
        power_sketch, inverse, precision=HIGHEST, preferred_element_type=jnp.float32
    )
    return (third_basis * jnp.sqrt(jnp.float32(H)), projection)


def solution(mesh):
    in_specs = (P("dp", "mp"), P("dp", "mp"), P("mp", None))
    out_specs = (P("mp", None), P(None, "mp"))
    return jax.shard_map(
        on_device, mesh=mesh, in_specs=in_specs, out_specs=out_specs, check_vma=False
    )
```

```python
import jax
import jax.numpy as jnp
from jax import lax
from jax.experimental import pallas as pl
from jax.sharding import PartitionSpec as P

H = 8192
K = 128
N_X = 4
N_Y = 8
N_MP = N_X * N_Y
N_DP = 16
X_GROUPS = [[y * N_X + x for x in range(N_X)] for y in range(N_Y)]
Y_GROUPS = [[y * N_X + x for y in range(N_Y)] for x in range(N_X)]
HIGHEST = lax.Precision.HIGHEST

def inverse_factor(gram_ref, inverse_ref):
    groups = [gram_ref[8 * g:8 * g + 8, :] for g in range(K // 8)]
    lanes = lax.broadcasted_iota(jnp.int32, (1, K), 1)
    sublanes = lax.broadcasted_iota(jnp.int32, (8, 1), 0)
    for step in range(K):
        own, inner = step // 8, step % 8
        row = groups[own][inner:inner + 1, :]
        pivot = row[:, step:step + 1]
        left = jnp.where(lanes == step, 1.0, row)
        inverse_ref[step:step + 1, :] = jnp.where(lanes > step, 0.0, left) * lax.rsqrt(pivot)
        scaled = left * (1.0 / pivot)
        for g in range(own, K // 8):
            column = groups[g][:, step:step + 1]
            if g == own:
                if inner == 7:
                    continue
                column = jnp.where(sublanes > inner, column, 0.0)
                kept = jnp.where((lanes == step) & (sublanes > inner), 0.0, groups[g])
            else:
                kept = jnp.where(lanes == step, 0.0, groups[g])
            groups[g] = kept - column * scaled


def normalise_kernel(gram_ref, product_ref, rows_ref, inverse_ref):
    inverse_factor(gram_ref, inverse_ref)
    rows = lax.dot_general(
        product_ref[...], inverse_ref[...], (((1,), (1,)), ((), ())),
        precision=HIGHEST, preferred_element_type=jnp.float32,
    )
    rows_ref[...] = rows.astype(rows_ref.dtype)


def normalise(gram, product):
    tokens = product.shape[0]
    return pl.pallas_call(
        normalise_kernel,
        out_shape=(
            jax.ShapeDtypeStruct((tokens, K), jnp.bfloat16),
            jax.ShapeDtypeStruct((K, K), jnp.float32),
        ),
    )(gram, product)

def rows_product(left, right):
    return lax.dot_general(
        left, right, (((0,), (0,)), ((), ())), preferred_element_type=jnp.float32
    )


def split_two(matrix):
    high = matrix.astype(jnp.bfloat16)
    low = (matrix - high.astype(jnp.float32)).astype(jnp.bfloat16)
    return jnp.concatenate([high, low], axis=1)


def exchange(blocks, axis, groups=None):
    return lax.all_to_all(blocks, axis, 0, 0, axis_index_groups=groups)


def scatter_sum(blocks, axis, groups=None):
    return jnp.sum(exchange(blocks, axis, groups).astype(jnp.float32), axis=0)


def gather(block, axis, count, groups=None):
    return exchange(jnp.broadcast_to(block[None], (count,) + block.shape), axis, groups)


def sum_over_tokens(partial_value):
    rows, columns = partial_value.shape
    mine = scatter_sum(partial_value.reshape(N_DP, rows // N_DP, columns), "dp")
    return gather(mine, "dp", N_DP).reshape(rows, columns)


def token_rows_of(data, sketch):
    tokens = data.shape[0]
    gram = lax.dot_general(
        sketch, sketch, (((0,), (0,)), ((), ())), precision=HIGHEST,
        preferred_element_type=jnp.float32,
    )
    both = jnp.dot(data, split_two(sketch), preferred_element_type=jnp.float32)
    product = both[:, :K] + both[:, K:]
    quarter, span = tokens // N_X, tokens // N_MP
    blocks = jnp.concatenate(
        [product.reshape(N_X, quarter, K), jnp.broadcast_to(gram[None], (N_X, K, K))], axis=1
    )
    mine = scatter_sum(blocks, "mp", X_GROUPS)
    blocks = jnp.concatenate(
        [mine[:quarter].reshape(N_Y, span, K), mine[quarter:].reshape(N_Y, K // N_Y, K)], axis=1
    )
    mine = gather(scatter_sum(blocks, "mp", Y_GROUPS), "mp", N_Y, Y_GROUPS)
    rows, inverse = normalise(
        mine[:, span:].reshape(K, K), mine[:, :span].reshape(quarter, K)
    )
    return gather(rows, "mp", N_X, X_GROUPS).reshape(tokens, K), inverse


def on_device(activations, output_grads, probe_matrix):
    tokens = activations.shape[0]
    partial_value = jnp.dot(output_grads, probe_matrix, preferred_element_type=jnp.float32)
    mine = scatter_sum(partial_value.astype(jnp.bfloat16).reshape(N_MP, tokens // N_MP, K), "mp")
    probe_rows = gather(mine.astype(jnp.bfloat16), "mp", N_MP).reshape(tokens, K)

    sketch = sum_over_tokens(rows_product(activations, probe_rows))
    token_rows, _ = token_rows_of(activations, sketch)
    back_sketch = sum_over_tokens(rows_product(output_grads, token_rows))
    unit_rows, _ = token_rows_of(output_grads, back_sketch)
    power_sketch = sum_over_tokens(rows_product(activations, unit_rows))
    last_rows, inverse = token_rows_of(activations, power_sketch)
    projection = sum_over_tokens(rows_product(last_rows, output_grads))
    third_basis = lax.dot_general(
        power_sketch, inverse, (((1,), (1,)), ((), ())), precision=HIGHEST,
        preferred_element_type=jnp.float32,
    )
    return (third_basis * jnp.sqrt(jnp.float32(H)), projection)


def solution(mesh):
    in_specs = (P("dp", "mp"), P("dp", "mp"), P("mp", None))
    out_specs = (P("mp", None), P(None, "mp"))
    return jax.shard_map(
        on_device, mesh=mesh, in_specs=in_specs, out_specs=out_specs, check_vma=False
    )
```

```python
import jax
import jax.numpy as jnp
from jax import lax
from jax.experimental import pallas as pl
from jax.experimental.pallas import tpu as pltpu
from jax.sharding import PartitionSpec as P

H = 8192
K = 128
N_X = 4
N_Y = 8
N_MP = N_X * N_Y
N_DP = 16
X_GROUPS = [[y * N_X + x for x in range(N_X)] for y in range(N_Y)]
Y_GROUPS = [[y * N_X + x for y in range(N_Y)] for x in range(N_X)]
HIGHEST = lax.Precision.HIGHEST


def spread(value):
    return jnp.broadcast_to(value, (8, K))


def inverse_factor(groups, inverse_ref):
    lanes = lax.broadcasted_iota(jnp.int32, (8, K), 1)
    for own in range(K // 8):
        first = 8 * own
        rows = [spread(groups[own][j:j + 1, :]) for j in range(8)]
        inner = [
            [spread(rows[i][:, first + j:first + j + 1]) for j in range(i + 1)] for i in range(8)
        ]
        factor = [[None] * 8 for _ in range(8)]
        inverse_pivots = []
        for j in range(8):
            inverse_pivots.append(1.0 / inner[j][j])
            for i in range(j + 1, 8):
                factor[i][j] = inner[i][j] * inverse_pivots[j]
            for i in range(j + 1, 8):
                for m in range(j + 1, i + 1):
                    inner[i][m] = inner[i][m] - factor[i][j] * inner[m][j]
        inside = (lanes >= first) & (lanes < first + 8)
        done = []
        for j in range(8):
            row = jnp.where(inside, jnp.where(lanes == first + j, 1.0, 0.0), rows[j])
            for m in range(j):
                row = row - factor[j][m] * done[m]
            done.append(row)
            scaled = jnp.where(lanes > first + j, 0.0, row * lax.rsqrt(inner[j][j]))
            inverse_ref[first + j:first + j + 1, :] = scaled[0:1, :]
        for g in range(own + 1, K // 8):
            kept = jnp.where(inside, 0.0, groups[g])
            columns = []
            for j in range(8):
                column = spread(groups[g][:, first + j:first + j + 1])
                for m in range(j):
                    column = column - columns[m] * factor[j][m]
                columns.append(column)
            for j in range(8):
                kept = kept - (columns[j] * inverse_pivots[j]) * done[j]
            groups[g] = kept


def normalise_kernel(pieces_ref, rows_ref, inverse_ref):
    span = pieces_ref.shape[1] - K // N_Y
    groups = []
    for y in range(N_Y):
        for start in range(span, pieces_ref.shape[1], 8):
            groups.append(pieces_ref[y, start:start + 8, :])
    inverse_factor(groups, inverse_ref)
    for y in range(N_Y):
        rows = lax.dot_general(
            pieces_ref[y, :span, :], inverse_ref[...], (((1,), (1,)), ((), ())),
            precision=HIGHEST, preferred_element_type=jnp.float32,
        ).astype(rows_ref.dtype)
        for x in range(N_X):
            rows_ref[x, span * y:span * (y + 1), :] = rows


def normalise(pieces):
    span = pieces.shape[1] - K // N_Y
    return pl.pallas_call(
        normalise_kernel,
        out_shape=(
            jax.ShapeDtypeStruct((N_X, N_Y * span, K), jnp.bfloat16),
            jax.ShapeDtypeStruct((K, K), jnp.float32),
        ),
        compiler_params=pltpu.CompilerParams(vmem_limit_bytes=16 << 20),
    )(pieces)


def rows_product(left, right):
    return lax.dot_general(
        left, right, (((0,), (0,)), ((), ())), preferred_element_type=jnp.float32
    )


def split_two(matrix):
    high = matrix.astype(jnp.bfloat16)
    low = (matrix - high.astype(jnp.float32)).astype(jnp.bfloat16)
    return jnp.concatenate([high, low], axis=1)


def exchange(blocks, axis, groups=None):
    return lax.all_to_all(blocks, axis, 0, 0, axis_index_groups=groups)


def scatter_sum(blocks, axis, groups=None):
    return jnp.sum(exchange(blocks, axis, groups).astype(jnp.float32), axis=0)


def gather(block, axis, count, groups=None):
    return exchange(jnp.broadcast_to(block[None], (count,) + block.shape), axis, groups)


def sum_over_tokens(partial_value):
    rows, columns = partial_value.shape
    mine = scatter_sum(partial_value.reshape(N_DP, rows // N_DP, columns), "dp")
    if mine.size * 4 * N_DP > 1 << 18:
        return lax.all_gather(mine, "dp", tiled=True)
    return gather(mine, "dp", N_DP).reshape(rows, columns)


def token_rows_of(data, sketch):
    tokens = data.shape[0]
    gram = lax.dot_general(
        sketch, sketch, (((0,), (0,)), ((), ())), precision=HIGHEST,
        preferred_element_type=jnp.float32,
    )
    both = jnp.dot(data, split_two(sketch), preferred_element_type=jnp.float32)
    product = both[:, :K] + both[:, K:]
    quarter, span = tokens // N_X, tokens // N_MP
    blocks = jnp.concatenate(
        [product.reshape(N_X, quarter, K), jnp.broadcast_to(gram[None], (N_X, K, K))], axis=1
    )
    mine = scatter_sum(blocks, "mp", X_GROUPS)
    blocks = jnp.concatenate(
        [mine[:quarter].reshape(N_Y, span, K), mine[quarter:].reshape(N_Y, K // N_Y, K)], axis=1
    )
    mine = gather(scatter_sum(blocks, "mp", Y_GROUPS), "mp", N_Y, Y_GROUPS)
    rows, inverse = normalise(mine)
    return exchange(rows, "mp", X_GROUPS).reshape(tokens, K), inverse


def on_device(activations, output_grads, probe_matrix):
    tokens = activations.shape[0]
    partial_value = jnp.dot(output_grads, probe_matrix, preferred_element_type=jnp.float32)
    mine = scatter_sum(partial_value.astype(jnp.bfloat16).reshape(N_MP, tokens // N_MP, K), "mp")
    probe_rows = gather(mine.astype(jnp.bfloat16), "mp", N_MP).reshape(tokens, K)

    sketch = sum_over_tokens(rows_product(activations, probe_rows))
    token_rows, _ = token_rows_of(activations, sketch)
    back_sketch = sum_over_tokens(rows_product(output_grads, token_rows))
    unit_rows, _ = token_rows_of(output_grads, back_sketch)
    power_sketch = sum_over_tokens(rows_product(activations, unit_rows))
    last_rows, inverse = token_rows_of(activations, power_sketch)
    partial_value = rows_product(last_rows, output_grads).reshape(N_DP, K // N_DP, -1)
    mine = scatter_sum(partial_value, "dp").astype(jnp.bfloat16)
    projection = lax.all_gather(mine, "dp", tiled=True).astype(jnp.float32)
    third_basis = lax.dot_general(
        power_sketch, inverse, (((1,), (1,)), ((), ())), precision=HIGHEST,
        preferred_element_type=jnp.float32,
    )
    return (third_basis * jnp.sqrt(jnp.float32(H)), projection)


def solution(mesh):
    in_specs = (P("dp", "mp"), P("dp", "mp"), P("mp", None))
    out_specs = (P("mp", None), P(None, "mp"))
    return jax.shard_map(
        on_device, mesh=mesh, in_specs=in_specs, out_specs=out_specs, check_vma=False
    )
```

```python
import jax
import jax.numpy as jnp
from jax import lax
from jax.experimental import pallas as pl
from jax.experimental.pallas import tpu as pltpu
from jax.sharding import PartitionSpec as P

H = 8192
K = 128
N_X = 4
N_Y = 8
N_MP = N_X * N_Y
N_CORE = 2
N_Z = 8
N_DP = N_Z * N_CORE
X_GROUPS = [[y * N_X + x for x in range(N_X)] for y in range(N_Y)]
Y_GROUPS = [[y * N_X + x for y in range(N_Y)] for x in range(N_X)]
CORE_GROUPS = [[z * N_CORE + core for core in range(N_CORE)] for z in range(N_Z)]
Z_GROUPS = [[z * N_CORE + core for z in range(N_Z)] for core in range(N_CORE)]
HIGHEST = lax.Precision.HIGHEST


def spread(value):
    return jnp.broadcast_to(value, (8, K))


def inverse_factor(groups, inverse_ref):
    lanes = lax.broadcasted_iota(jnp.int32, (8, K), 1)
    for own in range(K // 8):
        first = 8 * own
        rows = [spread(groups[own][j:j + 1, :]) for j in range(8)]
        inner = [
            [spread(rows[i][:, first + j:first + j + 1]) for j in range(i + 1)] for i in range(8)
        ]
        factor = [[None] * 8 for _ in range(8)]
        inverse_pivots = []
        for j in range(8):
            inverse_pivots.append(1.0 / inner[j][j])
            for i in range(j + 1, 8):
                factor[i][j] = inner[i][j] * inverse_pivots[j]
            for i in range(j + 1, 8):
                for m in range(j + 1, i + 1):
                    inner[i][m] = inner[i][m] - factor[i][j] * inner[m][j]
        inside = (lanes >= first) & (lanes < first + 8)
        done = []
        for j in range(8):
            row = jnp.where(inside, jnp.where(lanes == first + j, 1.0, 0.0), rows[j])
            for m in range(j):
                row = row - factor[j][m] * done[m]
            done.append(row)
            scaled = jnp.where(lanes > first + j, 0.0, row * lax.rsqrt(inner[j][j]))
            inverse_ref[first + j:first + j + 1, :] = scaled[0:1, :]
        for g in range(own + 1, K // 8):
            kept = jnp.where(inside, 0.0, groups[g])
            columns = []
            for j in range(8):
                column = spread(groups[g][:, first + j:first + j + 1])
                for m in range(j):
                    column = column - columns[m] * factor[j][m]
                columns.append(column)
            for j in range(8):
                kept = kept - (columns[j] * inverse_pivots[j]) * done[j]
            groups[g] = kept


def normalise_kernel(pieces_ref, rows_ref, inverse_ref):
    span = pieces_ref.shape[1] - K // N_Y
    groups = []
    for y in range(N_Y):
        for start in range(span, pieces_ref.shape[1], 8):
            groups.append(pieces_ref[y, start:start + 8, :])
    inverse_factor(groups, inverse_ref)
    for y in range(N_Y):
        rows = lax.dot_general(
            pieces_ref[y, :span, :], inverse_ref[...], (((1,), (1,)), ((), ())),
            precision=HIGHEST, preferred_element_type=jnp.float32,
        ).astype(rows_ref.dtype)
        for x in range(N_X):
            rows_ref[x, span * y:span * (y + 1), :] = rows


def normalise(pieces):
    span = pieces.shape[1] - K // N_Y
    return pl.pallas_call(
        normalise_kernel,
        out_shape=(
            jax.ShapeDtypeStruct((N_X, N_Y * span, K), jnp.bfloat16),
            jax.ShapeDtypeStruct((K, K), jnp.float32),
        ),
        compiler_params=pltpu.CompilerParams(vmem_limit_bytes=16 << 20),
    )(pieces)


def rows_product(left, right):
    return lax.dot_general(
        left, right, (((0,), (0,)), ((), ())), preferred_element_type=jnp.float32
    )


def split_two(matrix):
    high = matrix.astype(jnp.bfloat16)
    low = (matrix - high.astype(jnp.float32)).astype(jnp.bfloat16)
    return jnp.concatenate([high, low], axis=1)


def exchange(blocks, axis, groups=None):
    return lax.all_to_all(blocks, axis, 0, 0, axis_index_groups=groups)


def scatter_sum(blocks, axis, groups=None):
    return jnp.sum(exchange(blocks, axis, groups).astype(jnp.float32), axis=0)


def gather(block, axis, count, groups=None):
    return exchange(jnp.broadcast_to(block[None], (count,) + block.shape), axis, groups)


def sum_over_tokens(partial_value):
    rows, columns = partial_value.shape
    mine = scatter_sum(partial_value.reshape(N_DP, rows // N_DP, columns), "dp")
    return gather(mine, "dp", N_DP).reshape(rows, columns)


def staged_sum_over_tokens(partial_value, held_as):
    rows, columns = partial_value.shape
    half = rows // N_CORE
    mine = scatter_sum(partial_value.reshape(N_CORE, half, columns), "dp", CORE_GROUPS)
    mine = scatter_sum(mine.reshape(N_Z, half // N_Z, columns), "dp", Z_GROUPS)
    mine = gather(mine.astype(held_as), "dp", N_Z, Z_GROUPS).reshape(half, columns)
    return lax.all_gather(mine, "dp", axis_index_groups=CORE_GROUPS, tiled=True)


def token_rows_of(data, sketch):
    tokens = data.shape[0]
    gram = lax.dot_general(
        sketch, sketch, (((0,), (0,)), ((), ())), precision=HIGHEST,
        preferred_element_type=jnp.float32,
    )
    both = jnp.dot(data, split_two(sketch), preferred_element_type=jnp.float32)
    product = both[:, :K] + both[:, K:]
    quarter, span = tokens // N_X, tokens // N_MP
    blocks = jnp.concatenate(
        [product.reshape(N_X, quarter, K), jnp.broadcast_to(gram[None], (N_X, K, K))], axis=1
    )
    mine = scatter_sum(blocks, "mp", X_GROUPS)
    blocks = jnp.concatenate(
        [mine[:quarter].reshape(N_Y, span, K), mine[quarter:].reshape(N_Y, K // N_Y, K)], axis=1
    )
    mine = gather(scatter_sum(blocks, "mp", Y_GROUPS), "mp", N_Y, Y_GROUPS)
    rows, inverse = normalise(mine)
    return exchange(rows, "mp", X_GROUPS).reshape(tokens, K), inverse


def on_device(activations, output_grads, probe_matrix):
    tokens = activations.shape[0]
    partial_value = jnp.dot(output_grads, probe_matrix, preferred_element_type=jnp.float32)
    mine = scatter_sum(partial_value.astype(jnp.bfloat16).reshape(N_MP, tokens // N_MP, K), "mp")
    probe_rows = gather(mine.astype(jnp.bfloat16), "mp", N_MP).reshape(tokens, K)

    sketch = sum_over_tokens(rows_product(activations, probe_rows))
    token_rows, _ = token_rows_of(activations, sketch)
    back_sketch = staged_sum_over_tokens(rows_product(output_grads, token_rows), jnp.float32)
    unit_rows, _ = token_rows_of(output_grads, back_sketch)
    power_sketch = sum_over_tokens(rows_product(activations, unit_rows))
    last_rows, inverse = token_rows_of(activations, power_sketch)
    projection = staged_sum_over_tokens(rows_product(last_rows, output_grads), jnp.bfloat16)
    third_basis = lax.dot_general(
        power_sketch, inverse, (((1,), (1,)), ((), ())), precision=HIGHEST,
        preferred_element_type=jnp.float32,
    )
    return (third_basis * jnp.sqrt(jnp.float32(H)), projection.astype(jnp.float32))


def solution(mesh):
    in_specs = (P("dp", "mp"), P("dp", "mp"), P("mp", None))
    out_specs = (P("mp", None), P(None, "mp"))
    return jax.shard_map(
        on_device, mesh=mesh, in_specs=in_specs, out_specs=out_specs, check_vma=False
    )
```

```python
import jax
import jax.numpy as jnp
from jax import lax
from jax.experimental import pallas as pl
from jax.experimental.pallas import tpu as pltpu
from jax.sharding import PartitionSpec as P

H = 8192
K = 128
N_X = 4
N_Y = 8
N_MP = N_X * N_Y
PARTS = 3
N_CORE = 2
N_Z = 8
N_DP = N_Z * N_CORE
X_GROUPS = [[y * N_X + x for x in range(N_X)] for y in range(N_Y)]
Y_GROUPS = [[y * N_X + x for y in range(N_Y)] for x in range(N_X)]
CORE_GROUPS = [[z * N_CORE + core for core in range(N_CORE)] for z in range(N_Z)]
Z_GROUPS = [[z * N_CORE + core for z in range(N_Z)] for core in range(N_CORE)]
HIGHEST = lax.Precision.HIGHEST


def spread(value):
    return jnp.broadcast_to(value, (8, K))


def inverse_factor(groups, inverse_ref):
    lanes = lax.broadcasted_iota(jnp.int32, (8, K), 1)
    for own in range(K // 8):
        first = 8 * own
        rows = [spread(groups[own][j:j + 1, :]) for j in range(8)]
        inner = [
            [spread(rows[i][:, first + j:first + j + 1]) for j in range(i + 1)] for i in range(8)
        ]
        factor = [[None] * 8 for _ in range(8)]
        inverse_pivots = []
        for j in range(8):
            inverse_pivots.append(1.0 / inner[j][j])
            for i in range(j + 1, 8):
                factor[i][j] = inner[i][j] * inverse_pivots[j]
            for i in range(j + 1, 8):
                for m in range(j + 1, i + 1):
                    inner[i][m] = inner[i][m] - factor[i][j] * inner[m][j]
        inside = (lanes >= first) & (lanes < first + 8)
        done = []
        for j in range(8):
            row = jnp.where(inside, jnp.where(lanes == first + j, 1.0, 0.0), rows[j])
            for m in range(j):
                row = row - factor[j][m] * done[m]
            done.append(row)
            scaled = jnp.where(lanes > first + j, 0.0, row * lax.rsqrt(inner[j][j]))
            inverse_ref[first + j:first + j + 1, :] = scaled[0:1, :]
        for g in range(own + 1, K // 8):
            kept = jnp.where(inside, 0.0, groups[g])
            columns = []
            for j in range(8):
                column = spread(groups[g][:, first + j:first + j + 1])
                for m in range(j):
                    column = column - columns[m] * factor[j][m]
                columns.append(column)
            for j in range(8):
                kept = kept - (columns[j] * inverse_pivots[j]) * done[j]
            groups[g] = kept


def normalise_kernel(pieces_ref, rows_ref, inverse_ref):
    parts = 1 if pieces_ref.dtype == jnp.float32 else PARTS
    depth = K // N_Y
    span = pieces_ref.shape[1] - parts * depth
    groups = []
    for y in range(N_Y):
        whole = pieces_ref[y, span:span + depth, :].astype(jnp.float32)
        for part in range(1, parts):
            start = span + part * depth
            whole = whole + pieces_ref[y, start:start + depth, :].astype(jnp.float32)
        groups += [whole[start:start + 8, :] for start in range(0, depth, 8)]
    inverse_factor(groups, inverse_ref)
    for y in range(N_Y):
        rows = lax.dot_general(
            pieces_ref[y, :span, :].astype(jnp.float32), inverse_ref[...],
            (((1,), (1,)), ((), ())), precision=HIGHEST, preferred_element_type=jnp.float32,
        ).astype(rows_ref.dtype)
        for x in range(N_X):
            rows_ref[x, span * y:span * (y + 1), :] = rows


def normalise(pieces, span):
    return pl.pallas_call(
        normalise_kernel,
        out_shape=(
            jax.ShapeDtypeStruct((N_X, N_Y * span, K), jnp.bfloat16),
            jax.ShapeDtypeStruct((K, K), jnp.float32),
        ),
        compiler_params=pltpu.CompilerParams(vmem_limit_bytes=16 << 20),
    )(pieces)


def rows_product(left, right):
    return lax.dot_general(
        left, right, (((0,), (0,)), ((), ())), preferred_element_type=jnp.float32
    )


def split(matrix, count):
    parts = []
    for _ in range(count):
        high = lax.reduce_precision(matrix, 8, 7)
        parts.append(high.astype(jnp.bfloat16))
        matrix = matrix - high
    return parts


def exchange(blocks, axis, groups=None):
    return lax.all_to_all(blocks, axis, 0, 0, axis_index_groups=groups)


def scatter_sum(blocks, axis, groups=None):
    return jnp.sum(exchange(blocks, axis, groups).astype(jnp.float32), axis=0)


def gather(block, axis, count, groups=None):
    return exchange(jnp.broadcast_to(block[None], (count,) + block.shape), axis, groups)


def sum_over_tokens(partial_value):
    rows, columns = partial_value.shape
    mine = scatter_sum(partial_value.reshape(N_DP, rows // N_DP, columns), "dp")
    return gather(mine, "dp", N_DP).reshape(rows, columns)


def staged_sum_over_tokens(partial_value, held_as):
    rows, columns = partial_value.shape
    half = rows // N_CORE
    blocks = partial_value.reshape(N_CORE, N_Z, half // N_Z, columns).swapaxes(0, 1)
    mine = scatter_sum(blocks.reshape(N_DP, half // N_Z, columns), "dp")
    mine = gather(mine.astype(held_as), "dp", N_Z, Z_GROUPS).reshape(half, columns)
    return lax.all_gather(mine, "dp", axis_index_groups=CORE_GROUPS, tiled=True)


def token_rows_of(data, sketch, held_as):
    tokens = data.shape[0]
    parts = 1 if held_as == jnp.float32 else PARTS
    quarter, span, depth = tokens // N_X, tokens // N_MP, K // N_Y

    def parts_of(gram):
        return [gram] if parts == 1 else split(gram, parts)

    def total(received, rows):
        received = received.astype(jnp.float32)
        pieces = received[:, rows:].reshape(received.shape[0], parts, -1, K)
        return jnp.sum(received[:, :rows], axis=0), jnp.sum(jnp.sum(pieces, axis=1), axis=0)

    gram = lax.dot_general(
        sketch, sketch, (((0,), (0,)), ((), ())), precision=HIGHEST,
        preferred_element_type=jnp.float32,
    )
    both = jnp.dot(
        data, jnp.concatenate(split(sketch, 2), axis=1), preferred_element_type=jnp.float32
    )
    product = (both[:, :K] + both[:, K:]).astype(held_as)
    blocks = jnp.concatenate(
        [product.reshape(N_X, quarter, K)]
        + [jnp.broadcast_to(part[None], (N_X, K, K)) for part in parts_of(gram)], axis=1
    )
    product, gram = total(exchange(blocks, "mp", X_GROUPS), quarter)
    blocks = jnp.concatenate(
        [product.astype(held_as).reshape(N_Y, span, K)]
        + [part.reshape(N_Y, depth, K) for part in parts_of(gram)], axis=1
    )
    product, gram = total(exchange(blocks, "mp", Y_GROUPS), span)
    pieces = jnp.concatenate([product.astype(held_as)] + parts_of(gram), axis=0)
    rows, inverse = normalise(gather(pieces, "mp", N_Y, Y_GROUPS), span)
    return exchange(rows, "mp", X_GROUPS).reshape(tokens, K), inverse


def on_device(activations, output_grads, probe_matrix):
    tokens = activations.shape[0]
    partial_value = jnp.dot(output_grads, probe_matrix, preferred_element_type=jnp.float32)
    partial_value = partial_value.astype(jnp.bfloat16).reshape(N_X, tokens // N_X, K)
    mine = scatter_sum(partial_value, "mp", X_GROUPS).astype(jnp.bfloat16)
    mine = scatter_sum(mine.reshape(N_Y, tokens // N_MP, K), "mp", Y_GROUPS).astype(jnp.bfloat16)
    mine = gather(mine, "mp", N_Y, Y_GROUPS).reshape(tokens // N_X, K)
    probe_rows = gather(mine, "mp", N_X, X_GROUPS).reshape(tokens, K)

    sketch = sum_over_tokens(rows_product(activations, probe_rows))
    token_rows, _ = token_rows_of(activations, sketch, jnp.float32)
    back_sketch = staged_sum_over_tokens(rows_product(output_grads, token_rows), jnp.float32)
    unit_rows, _ = token_rows_of(output_grads, back_sketch, jnp.float32)
    power_sketch = sum_over_tokens(rows_product(activations, unit_rows))
    last_rows, inverse = token_rows_of(activations, power_sketch, jnp.bfloat16)
    projection = staged_sum_over_tokens(rows_product(last_rows, output_grads), jnp.bfloat16)
    third_basis = lax.dot_general(
        power_sketch, inverse, (((1,), (1,)), ((), ())), precision=HIGHEST,
        preferred_element_type=jnp.float32,
    )
    return (third_basis * jnp.sqrt(jnp.float32(H)), projection.astype(jnp.float32))


def solution(mesh):
    in_specs = (P("dp", "mp"), P("dp", "mp"), P("mp", None))
    out_specs = (P("mp", None), P(None, "mp"))
    return jax.shard_map(
        on_device, mesh=mesh, in_specs=in_specs, out_specs=out_specs, check_vma=False
    )
```

```python
import functools

import jax
import jax.numpy as jnp
from jax import lax
from jax.experimental import pallas as pl
from jax.experimental.pallas import tpu as pltpu
from jax.sharding import PartitionSpec as P

H = 8192
K = 128
N_X = 4
N_Y = 8
N_MP = N_X * N_Y
PARTS = 3
CHUNKS = 8
N_CORE = 2
N_Z = 8
N_DP = N_Z * N_CORE
X_GROUPS = [[y * N_X + x for x in range(N_X)] for y in range(N_Y)]
Y_GROUPS = [[y * N_X + x for y in range(N_Y)] for x in range(N_X)]
CORE_GROUPS = [[z * N_CORE + core for core in range(N_CORE)] for z in range(N_Z)]
Z_GROUPS = [[z * N_CORE + core for z in range(N_Z)] for core in range(N_CORE)]
HIGHEST = lax.Precision.HIGHEST


def spread(value):
    return jnp.broadcast_to(value, (8, K))


def inverse_factor(groups, inverse_ref):
    lanes = lax.broadcasted_iota(jnp.int32, (8, K), 1)
    for own in range(K // 8):
        first = 8 * own
        rows = [spread(groups[own][j:j + 1, :]) for j in range(8)]
        inner = [
            [spread(rows[i][:, first + j:first + j + 1]) for j in range(i + 1)] for i in range(8)
        ]
        factor = [[None] * 8 for _ in range(8)]
        inverse_pivots = []
        for j in range(8):
            inverse_pivots.append(1.0 / inner[j][j])
            for i in range(j + 1, 8):
                factor[i][j] = inner[i][j] * inverse_pivots[j]
            for i in range(j + 1, 8):
                for m in range(j + 1, i + 1):
                    inner[i][m] = inner[i][m] - factor[i][j] * inner[m][j]
        inside = (lanes >= first) & (lanes < first + 8)
        done = []
        for j in range(8):
            row = jnp.where(inside, jnp.where(lanes == first + j, 1.0, 0.0), rows[j])
            for m in range(j):
                row = row - factor[j][m] * done[m]
            done.append(row)
            scaled = jnp.where(lanes > first + j, 0.0, row * lax.rsqrt(inner[j][j]))
            inverse_ref[first + j:first + j + 1, :] = scaled[0:1, :]
        for g in range(own + 1, K // 8):
            kept = jnp.where(inside, 0.0, groups[g])
            columns = []
            for j in range(8):
                column = spread(groups[g][:, first + j:first + j + 1])
                for m in range(j):
                    column = column - columns[m] * factor[j][m]
                columns.append(column)
            for j in range(8):
                kept = kept - (columns[j] * inverse_pivots[j]) * done[j]
            groups[g] = kept


def nt_product(left, right):
    return lax.dot_general(
        left, right, (((1,), (1,)), ((), ())), precision=HIGHEST,
        preferred_element_type=jnp.float32,
    )


def normalise_kernel(transposed, pieces_ref, rows_ref, inverse_ref):
    parts = 1 if pieces_ref.dtype == jnp.float32 else PARTS
    depth = K // N_Y
    span = pieces_ref.shape[1] - parts * depth
    groups = []
    for y in range(N_Y):
        whole = pieces_ref[y, span:span + depth, :].astype(jnp.float32)
        for part in range(1, parts):
            start = span + part * depth
            whole = whole + pieces_ref[y, start:start + depth, :].astype(jnp.float32)
        groups += [whole[start:start + 8, :] for start in range(0, depth, 8)]
    inverse_factor(groups, inverse_ref)
    for y in range(N_Y):
        product = pieces_ref[y, :span, :].astype(jnp.float32)
        spot = slice(span * y, span * (y + 1))
        if transposed:
            rows = nt_product(inverse_ref[...], product).astype(rows_ref.dtype)
        else:
            rows = nt_product(product, inverse_ref[...]).astype(rows_ref.dtype)
        for x in range(N_X):
            if transposed:
                rows_ref[x, :, spot] = rows
            else:
                rows_ref[x, spot, :] = rows


def normalise(pieces, span, transposed):
    quarter = N_Y * span
    shape = (N_X, K, quarter) if transposed else (N_X, quarter, K)
    return pl.pallas_call(
        functools.partial(normalise_kernel, transposed),
        out_shape=(
            jax.ShapeDtypeStruct(shape, jnp.bfloat16), jax.ShapeDtypeStruct((K, K), jnp.float32)
        ),
        compiler_params=pltpu.CompilerParams(vmem_limit_bytes=16 << 20),
    )(pieces)


def parts_in(matrix, count):
    parts = []
    for _ in range(count):
        parts.append(matrix.astype(jnp.bfloat16))
        matrix = matrix - parts[-1].astype(jnp.float32)
    return parts


def products_kernel(data_ref, sketch_ref, blocks_ref):
    tokens = data_ref.shape[0]
    quarter, chunk = tokens // N_X, tokens // CHUNKS
    sketch = sketch_ref[...]
    gram = lax.dot_general(
        sketch, sketch, (((0,), (0,)), ((), ())), precision=HIGHEST,
        preferred_element_type=jnp.float32,
    )
    whole = blocks_ref.dtype == jnp.float32
    for i, part in enumerate([gram] if whole else parts_in(gram, PARTS)):
        for x in range(N_X):
            blocks_ref[x, quarter + K * i:quarter + K * (i + 1), :] = part
    both = jnp.concatenate(parts_in(sketch, 2), axis=1)
    for i in range(CHUNKS):
        product = jnp.dot(
            data_ref[chunk * i:chunk * (i + 1), :], both, preferred_element_type=jnp.float32
        )
        product = product[:, :K] + product[:, K:]
        start = chunk * i % quarter
        blocks_ref[chunk * i // quarter, start:start + chunk, :] = product.astype(blocks_ref.dtype)


def product_blocks(data, sketch, held_as):
    rows = data.shape[0] // N_X + K * (1 if held_as == jnp.float32 else PARTS)
    return pl.pallas_call(
        products_kernel,
        out_shape=jax.ShapeDtypeStruct((N_X, rows, K), held_as),
        in_specs=[pl.BlockSpec(memory_space=pltpu.VMEM)] * 2,
        compiler_params=pltpu.CompilerParams(vmem_limit_bytes=24 << 20),
    )(data, sketch)


def projection_kernel(rows_ref, grads_ref, blocks_ref):
    quarter = rows_ref.shape[2]
    total = jnp.zeros((K, grads_ref.shape[1]), jnp.float32)
    for x in range(N_X):
        total = total + jnp.dot(
            rows_ref[x], grads_ref[quarter * x:quarter * (x + 1), :],
            preferred_element_type=jnp.float32,
        )
    depth = K // N_DP
    for z in range(N_Z):
        for core in range(N_CORE):
            start = (core * N_Z + z) * depth
            blocks_ref[z * N_CORE + core] = total[start:start + depth, :]


def projection_blocks(rows, grads):
    return pl.pallas_call(
        projection_kernel,
        out_shape=jax.ShapeDtypeStruct((N_DP, K // N_DP, grads.shape[1]), jnp.float32),
        in_specs=[pl.BlockSpec(memory_space=pltpu.VMEM)] * 2,
        compiler_params=pltpu.CompilerParams(vmem_limit_bytes=24 << 20),
    )(rows, grads)


def rows_product(left, right):
    return lax.dot_general(
        left, right, (((0,), (0,)), ((), ())), preferred_element_type=jnp.float32
    )


def split(matrix, count):
    parts = []
    for _ in range(count):
        high = lax.reduce_precision(matrix, 8, 7)
        parts.append(high.astype(jnp.bfloat16))
        matrix = matrix - high
    return parts


def exchange(blocks, axis, groups=None):
    return lax.all_to_all(blocks, axis, 0, 0, axis_index_groups=groups)


def scatter_sum(blocks, axis, groups=None):
    return jnp.sum(exchange(blocks, axis, groups).astype(jnp.float32), axis=0)


def gather(block, axis, count, groups=None):
    return exchange(jnp.broadcast_to(block[None], (count,) + block.shape), axis, groups)


def sum_over_tokens(partial_value):
    rows, columns = partial_value.shape
    mine = scatter_sum(partial_value.reshape(N_DP, rows // N_DP, columns), "dp")
    return gather(mine, "dp", N_DP).reshape(rows, columns)


def blocks_over_tokens(partial_value):
    rows, columns = partial_value.shape
    blocks = partial_value.reshape(N_CORE, N_Z, rows // N_DP, columns).swapaxes(0, 1)
    return blocks.reshape(N_DP, rows // N_DP, columns)


def staged_sum_over_tokens(blocks, held_as):
    mine = scatter_sum(blocks, "dp").astype(held_as)
    mine = gather(mine, "dp", N_Z, Z_GROUPS).reshape(-1, blocks.shape[2])
    return lax.all_gather(mine, "dp", axis_index_groups=CORE_GROUPS, tiled=True)


def token_rows_of(data, sketch, held_as, transposed):
    tokens = data.shape[0]
    parts = 1 if held_as == jnp.float32 else PARTS
    quarter, span, depth = tokens // N_X, tokens // N_MP, K // N_Y

    def parts_of(gram):
        return [gram] if parts == 1 else split(gram, parts)

    def total(received, rows):
        received = received.astype(jnp.float32)
        pieces = received[:, rows:].reshape(received.shape[0], parts, -1, K)
        return jnp.sum(received[:, :rows], axis=0), jnp.sum(jnp.sum(pieces, axis=1), axis=0)

    blocks = product_blocks(data, sketch, held_as)
    product, gram = total(exchange(blocks, "mp", X_GROUPS), quarter)
    blocks = jnp.concatenate(
        [product.astype(held_as).reshape(N_Y, span, K)]
        + [part.reshape(N_Y, depth, K) for part in parts_of(gram)], axis=1
    )
    product, gram = total(exchange(blocks, "mp", Y_GROUPS), span)
    pieces = jnp.concatenate([product.astype(held_as)] + parts_of(gram), axis=0)
    rows, inverse = normalise(gather(pieces, "mp", N_Y, Y_GROUPS), span, transposed)
    return exchange(rows, "mp", X_GROUPS), inverse


def on_device(activations, output_grads, probe_matrix):
    tokens = activations.shape[0]
    partial_value = jnp.dot(output_grads, probe_matrix, preferred_element_type=jnp.float32)
    partial_value = partial_value.astype(jnp.bfloat16).reshape(N_MP, tokens // N_MP, K)
    mine = scatter_sum(partial_value, "mp").astype(jnp.bfloat16)
    probe_rows = gather(mine, "mp", N_MP).reshape(tokens, K)

    sketch = sum_over_tokens(rows_product(activations, probe_rows))
    token_rows, _ = token_rows_of(activations, sketch, jnp.float32, False)
    partial_value = rows_product(output_grads, token_rows.reshape(tokens, K))
    back_sketch = staged_sum_over_tokens(blocks_over_tokens(partial_value), jnp.float32)
    unit_rows, _ = token_rows_of(output_grads, back_sketch, jnp.float32, False)
    power_sketch = sum_over_tokens(rows_product(activations, unit_rows.reshape(tokens, K)))
    last_rows, inverse = token_rows_of(activations, power_sketch, jnp.bfloat16, True)
    projection = staged_sum_over_tokens(projection_blocks(last_rows, output_grads), jnp.bfloat16)
    third_basis = lax.dot_general(
        power_sketch, inverse, (((1,), (1,)), ((), ())), precision=HIGHEST,
        preferred_element_type=jnp.float32,
    )
    return (third_basis * jnp.sqrt(jnp.float32(H)), projection.astype(jnp.float32))


def solution(mesh):
    in_specs = (P("dp", "mp"), P("dp", "mp"), P("mp", None))
    out_specs = (P("mp", None), P(None, "mp"))
    return jax.shard_map(
        on_device, mesh=mesh, in_specs=in_specs, out_specs=out_specs, check_vma=False
    )
```

```python
import functools

import jax
import jax.numpy as jnp
from jax import lax
from jax.experimental import pallas as pl
from jax.experimental.pallas import tpu as pltpu
from jax.sharding import PartitionSpec as P

H = 8192
K = 128
N_X = 4
N_Y = 8
N_MP = N_X * N_Y
PARTS = 3
CHUNKS = 8
N_CORE = 2
N_Z = 8
N_DP = N_Z * N_CORE
X_GROUPS = [[y * N_X + x for x in range(N_X)] for y in range(N_Y)]
Y_GROUPS = [[y * N_X + x for y in range(N_Y)] for x in range(N_X)]
CORE_GROUPS = [[z * N_CORE + core for core in range(N_CORE)] for z in range(N_Z)]
Z_GROUPS = [[z * N_CORE + core for z in range(N_Z)] for core in range(N_CORE)]
HIGHEST = lax.Precision.HIGHEST
VMEM_SPEC = pl.BlockSpec(memory_space=pltpu.VMEM)


def spread(value):
    return jnp.broadcast_to(value, (8, K))


def inverse_factor(groups, inverse_ref):
    lanes = lax.broadcasted_iota(jnp.int32, (8, K), 1)
    for own in range(K // 8):
        first = 8 * own
        rows = [spread(groups[own][j:j + 1, :]) for j in range(8)]
        inner = [
            [spread(rows[i][:, first + j:first + j + 1]) for j in range(i + 1)] for i in range(8)
        ]
        factor = [[None] * 8 for _ in range(8)]
        inverse_pivots = []
        for j in range(8):
            inverse_pivots.append(1.0 / inner[j][j])
            for i in range(j + 1, 8):
                factor[i][j] = inner[i][j] * inverse_pivots[j]
            for i in range(j + 1, 8):
                for m in range(j + 1, i + 1):
                    inner[i][m] = inner[i][m] - factor[i][j] * inner[m][j]
        inside = (lanes >= first) & (lanes < first + 8)
        done = []
        for j in range(8):
            row = jnp.where(inside, jnp.where(lanes == first + j, 1.0, 0.0), rows[j])
            for m in range(j):
                row = row - factor[j][m] * done[m]
            done.append(row)
            scaled = jnp.where(lanes > first + j, 0.0, row * lax.rsqrt(inner[j][j]))
            inverse_ref[first + j:first + j + 1, :] = scaled[0:1, :]
        for g in range(own + 1, K // 8):
            kept = jnp.where(inside, 0.0, groups[g])
            columns = []
            for j in range(8):
                column = spread(groups[g][:, first + j:first + j + 1])
                for m in range(j):
                    column = column - columns[m] * factor[j][m]
                columns.append(column)
            for j in range(8):
                kept = kept - (columns[j] * inverse_pivots[j]) * done[j]
            groups[g] = kept


def nt_product(left, right):
    return lax.dot_general(
        left, right, (((1,), (1,)), ((), ())), precision=HIGHEST,
        preferred_element_type=jnp.float32,
    )


def gram_groups(pieces_ref, span):
    parts = 1 if pieces_ref.dtype == jnp.float32 else PARTS
    depth = K // N_Y
    groups = []
    for y in range(N_Y):
        whole = pieces_ref[y, span:span + depth, :].astype(jnp.float32)
        for part in range(1, parts):
            start = span + part * depth
            whole = whole + pieces_ref[y, start:start + depth, :].astype(jnp.float32)
        groups += [whole[start:start + 8, :] for start in range(0, depth, 8)]
    return groups


def inverse_kernel(span, pieces_ref, inverse_ref):
    inverse_factor(gram_groups(pieces_ref, span), inverse_ref)


def inverse_of(pieces, span):
    return pl.pallas_call(
        functools.partial(inverse_kernel, span),
        out_shape=jax.ShapeDtypeStruct((K, K), jnp.float32),
        in_specs=[VMEM_SPEC],
        compiler_params=pltpu.CompilerParams(vmem_limit_bytes=16 << 20),
        cost_estimate=pl.CostEstimate(
            flops=4 * K ** 3, bytes_accessed=pieces.size * 2 + 4 * K * K, transcendentals=K
        ),
    )(pieces)


def normalise_kernel(span, pieces_ref, rows_ref, inverse_ref):
    inverse_factor(gram_groups(pieces_ref, span), inverse_ref)
    for y in range(N_Y):
        rows = nt_product(pieces_ref[y, :span, :], inverse_ref[...]).astype(rows_ref.dtype)
        for x in range(N_X):
            rows_ref[x, span * y:span * (y + 1), :] = rows


def normalise(pieces, span):
    return pl.pallas_call(
        functools.partial(normalise_kernel, span),
        out_shape=(
            jax.ShapeDtypeStruct((N_X, N_Y * span, K), jnp.bfloat16),
            jax.ShapeDtypeStruct((K, K), jnp.float32),
        ),
        compiler_params=pltpu.CompilerParams(vmem_limit_bytes=16 << 20),
    )(pieces)


def parts_in(matrix, count):
    parts = []
    for _ in range(count):
        parts.append(matrix.astype(jnp.bfloat16))
        matrix = matrix - parts[-1].astype(jnp.float32)
    return parts


def streaming(kernel):
    def streamed(wide_ref, *refs):
        refs, held_ref, arrived = refs[:-2], refs[-2], refs[-1]
        chunk = wide_ref.shape[0] // CHUNKS
        copies = []
        for i in range(CHUNKS):
            rows = pl.ds(chunk * i, chunk)
            copies.append(
                pltpu.make_async_copy(wide_ref.at[rows], held_ref.at[rows], arrived.at[i])
            )
            copies[i].start()

        def wide(i):
            copies[i].wait()
            return held_ref[chunk * i:chunk * (i + 1), :]

        kernel(wide, *refs)

    return streamed


def call_streaming(kernel, out_shape, wide, *others):
    return pl.pallas_call(
        streaming(kernel),
        out_shape=out_shape,
        in_specs=[pl.BlockSpec(memory_space=pltpu.HBM)] + [VMEM_SPEC] * len(others),
        scratch_shapes=[
            pltpu.VMEM(wide.shape, wide.dtype), pltpu.SemaphoreType.DMA((CHUNKS,))
        ],
        compiler_params=pltpu.CompilerParams(vmem_limit_bytes=51 << 20),
    )(wide, *others)


def probe_kernel(wide, probe_ref, product_ref):
    chunk = product_ref.shape[0] // CHUNKS
    for i in range(CHUNKS):
        product = jnp.dot(wide(i), probe_ref[...], preferred_element_type=jnp.float32)
        product_ref[chunk * i:chunk * (i + 1), :] = product.astype(product_ref.dtype)


def products_kernel(wide, sketch_ref, blocks_ref):
    whole = blocks_ref.dtype == jnp.float32
    quarter = blocks_ref.shape[1] - K * (1 if whole else PARTS)
    chunk = N_X * quarter // CHUNKS
    sketch = sketch_ref[...]
    gram = lax.dot_general(
        sketch, sketch, (((0,), (0,)), ((), ())), precision=HIGHEST,
        preferred_element_type=jnp.float32,
    )
    for i, part in enumerate([gram] if whole else parts_in(gram, PARTS)):
        for x in range(N_X):
            blocks_ref[x, quarter + K * i:quarter + K * (i + 1), :] = part
    both = jnp.concatenate(parts_in(sketch, 2), axis=1)
    for i in range(CHUNKS):
        product = jnp.dot(wide(i), both, preferred_element_type=jnp.float32)
        product = product[:, :K] + product[:, K:]
        start = chunk * i % quarter
        blocks_ref[chunk * i // quarter, start:start + chunk, :] = product.astype(blocks_ref.dtype)


def resident_products_kernel(data_ref, sketch_ref, blocks_ref):
    chunk = data_ref.shape[0] // CHUNKS
    products_kernel(lambda i: data_ref[chunk * i:chunk * (i + 1), :], sketch_ref, blocks_ref)


def product_blocks(data, sketch, held_as, streamed):
    rows = data.shape[0] // N_X + K * (1 if held_as == jnp.float32 else PARTS)
    out_shape = jax.ShapeDtypeStruct((N_X, rows, K), held_as)
    if streamed:
        return call_streaming(products_kernel, out_shape, data, sketch)
    return pl.pallas_call(
        resident_products_kernel,
        out_shape=out_shape,
        in_specs=[VMEM_SPEC] * 2,
        compiler_params=pltpu.CompilerParams(vmem_limit_bytes=24 << 20),
    )(data, sketch)


def projection_kernel(wide, rows_ref, inverse_ref, blocks_ref):
    quarter = rows_ref.shape[1]
    chunk = N_X * quarter // CHUNKS
    total = jnp.zeros((K, blocks_ref.shape[2]), jnp.float32)
    for i in range(CHUNKS):
        start = chunk * i % quarter
        rows = rows_ref[chunk * i // quarter, start:start + chunk, :]
        total = total + lax.dot_general(
            rows, wide(i), (((0,), (0,)), ((), ())), preferred_element_type=jnp.float32
        )
    total = jnp.dot(
        inverse_ref[...], total, precision=HIGHEST, preferred_element_type=jnp.float32
    )
    depth = K // N_DP
    for z in range(N_Z):
        for core in range(N_CORE):
            start = (core * N_Z + z) * depth
            blocks_ref[z * N_CORE + core] = total[start:start + depth, :]


def rows_product(left, right):
    return lax.dot_general(
        left, right, (((0,), (0,)), ((), ())), preferred_element_type=jnp.float32
    )


def split(matrix, count):
    parts = []
    for _ in range(count):
        high = lax.reduce_precision(matrix, 8, 7)
        parts.append(high.astype(jnp.bfloat16))
        matrix = matrix - high
    return parts


def exchange(blocks, axis, groups=None):
    return lax.all_to_all(blocks, axis, 0, 0, axis_index_groups=groups)


def scatter_sum(blocks, axis, groups=None):
    return jnp.sum(exchange(blocks, axis, groups).astype(jnp.float32), axis=0)


def gather(block, axis, count, groups=None):
    return exchange(jnp.broadcast_to(block[None], (count,) + block.shape), axis, groups)


def sum_over_tokens(partial_value):
    rows, columns = partial_value.shape
    mine = scatter_sum(partial_value.reshape(N_DP, rows // N_DP, columns), "dp")
    return gather(mine, "dp", N_DP).reshape(rows, columns)


def blocks_over_tokens(partial_value):
    rows, columns = partial_value.shape
    blocks = partial_value.reshape(N_CORE, N_Z, rows // N_DP, columns).swapaxes(0, 1)
    return blocks.reshape(N_DP, rows // N_DP, columns)


def staged_sum_over_tokens(blocks, held_as):
    mine = scatter_sum(blocks, "dp").astype(held_as)
    mine = gather(mine, "dp", N_Z, Z_GROUPS).reshape(-1, blocks.shape[2]).astype(jnp.float32)
    return lax.all_gather(mine, "dp", axis_index_groups=CORE_GROUPS, tiled=True)


def token_sums_of(data, sketch, held_as, streamed):
    tokens = data.shape[0]
    parts = 1 if held_as == jnp.float32 else PARTS
    quarter, span, depth = tokens // N_X, tokens // N_MP, K // N_Y

    def parts_of(gram):
        return [gram] if parts == 1 else split(gram, parts)

    def total(received, rows):
        received = received.astype(jnp.float32)
        pieces = received[:, rows:].reshape(received.shape[0], parts, -1, K)
        return jnp.sum(received[:, :rows], axis=0), jnp.sum(jnp.sum(pieces, axis=1), axis=0)

    blocks = product_blocks(data, sketch, held_as, streamed)
    product, gram = total(exchange(blocks, "mp", X_GROUPS), quarter)
    blocks = jnp.concatenate(
        [product.astype(held_as).reshape(N_Y, span, K)]
        + [part.reshape(N_Y, depth, K) for part in parts_of(gram)], axis=1
    )
    product, gram = total(exchange(blocks, "mp", Y_GROUPS), span)
    pieces = jnp.concatenate([product.astype(held_as)] + parts_of(gram), axis=0)
    return gather(pieces, "mp", N_Y, Y_GROUPS), span


def token_rows_of(data, sketch, streamed):
    rows, _ = normalise(*token_sums_of(data, sketch, jnp.float32, streamed))
    return exchange(rows, "mp", X_GROUPS).reshape(data.shape[0], K)


def on_device(activations, output_grads, probe_matrix):
    tokens = activations.shape[0]
    partial_value = call_streaming(
        probe_kernel, jax.ShapeDtypeStruct((tokens, K), jnp.bfloat16), output_grads, probe_matrix
    )
    mine = scatter_sum(partial_value.reshape(N_MP, tokens // N_MP, K), "mp").astype(jnp.bfloat16)
    probe_rows = gather(mine, "mp", N_MP).reshape(tokens, K)

    sketch = sum_over_tokens(rows_product(activations, probe_rows))
    token_rows = token_rows_of(activations, sketch, False)
    partial_value = rows_product(output_grads, token_rows)
    back_sketch = staged_sum_over_tokens(blocks_over_tokens(partial_value), jnp.float32)
    unit_rows = token_rows_of(output_grads, back_sketch, True)
    power_sketch = sum_over_tokens(rows_product(activations, unit_rows))
    pieces, span = token_sums_of(activations, power_sketch, jnp.bfloat16, False)
    inverse = inverse_of(pieces, span)
    products = gather(pieces[:, :span].reshape(tokens // N_X, K), "mp", N_X, X_GROUPS)
    blocks = call_streaming(
        projection_kernel,
        jax.ShapeDtypeStruct((N_DP, K // N_DP, output_grads.shape[1]), jnp.float32),
        output_grads, products, inverse,
    )
    projection = staged_sum_over_tokens(blocks, jnp.bfloat16)
    third_basis = lax.dot_general(
        power_sketch, inverse, (((1,), (1,)), ((), ())), precision=HIGHEST,
        preferred_element_type=jnp.float32,
    )
    return (third_basis * jnp.sqrt(jnp.float32(H)), projection)


def solution(mesh):
    in_specs = (P("dp", "mp"), P("dp", "mp"), P("mp", None))
    out_specs = (P("mp", None), P(None, "mp"))
    return jax.shard_map(
        on_device, mesh=mesh, in_specs=in_specs, out_specs=out_specs, check_vma=False
    )
```

```python
import functools

import jax
import jax.numpy as jnp
from jax import lax
from jax.experimental import pallas as pl
from jax.experimental.pallas import tpu as pltpu
from jax.sharding import PartitionSpec as P

H = 8192
K = 128
N_X = 4
N_Y = 8
N_MP = N_X * N_Y
PARTS = 3
CHUNKS = 8
N_CORE = 2
N_Z = 8
N_DP = N_Z * N_CORE
X_GROUPS = [[y * N_X + x for x in range(N_X)] for y in range(N_Y)]
Y_GROUPS = [[y * N_X + x for y in range(N_Y)] for x in range(N_X)]
CORE_GROUPS = [[z * N_CORE + core for core in range(N_CORE)] for z in range(N_Z)]
Z_GROUPS = [[z * N_CORE + core for z in range(N_Z)] for core in range(N_CORE)]
HIGHEST = lax.Precision.HIGHEST
VMEM_SPEC = pl.BlockSpec(memory_space=pltpu.VMEM)


def spread(value):
    return jnp.broadcast_to(value, (8, K))


def inverse_factor(groups, inverse_ref):
    lanes = lax.broadcasted_iota(jnp.int32, (8, K), 1)
    for own in range(K // 8):
        first = 8 * own
        rows = [spread(groups[own][j:j + 1, :]) for j in range(8)]
        inner = [
            [spread(rows[i][:, first + j:first + j + 1]) for j in range(i + 1)] for i in range(8)
        ]
        factor = [[None] * 8 for _ in range(8)]
        inverse_pivots = []
        for j in range(8):
            inverse_pivots.append(1.0 / inner[j][j])
            for i in range(j + 1, 8):
                factor[i][j] = inner[i][j] * inverse_pivots[j]
            for i in range(j + 1, 8):
                for m in range(j + 1, i + 1):
                    inner[i][m] = inner[i][m] - factor[i][j] * inner[m][j]
        inside = (lanes >= first) & (lanes < first + 8)
        done = []
        for j in range(8):
            row = jnp.where(inside, jnp.where(lanes == first + j, 1.0, 0.0), rows[j])
            for m in range(j):
                row = row - factor[j][m] * done[m]
            done.append(row)
            scaled = jnp.where(lanes > first + j, 0.0, row * lax.rsqrt(inner[j][j]))
            inverse_ref[first + j:first + j + 1, :] = scaled[0:1, :]
        for g in range(own + 1, K // 8):
            kept = jnp.where(inside, 0.0, groups[g])
            columns = []
            for j in range(8):
                column = spread(groups[g][:, first + j:first + j + 1])
                for m in range(j):
                    column = column - columns[m] * factor[j][m]
                columns.append(column)
            for j in range(8):
                kept = kept - (columns[j] * inverse_pivots[j]) * done[j]
            groups[g] = kept


def nt_product(left, right):
    return lax.dot_general(
        left, right, (((1,), (1,)), ((), ())), precision=HIGHEST,
        preferred_element_type=jnp.float32,
    )


def gram_groups(pieces_ref, span):
    parts = 1 if pieces_ref.dtype == jnp.float32 else PARTS
    depth = K // N_Y
    groups = []
    for y in range(N_Y):
        whole = pieces_ref[y, span:span + depth, :].astype(jnp.float32)
        for part in range(1, parts):
            start = span + part * depth
            whole = whole + pieces_ref[y, start:start + depth, :].astype(jnp.float32)
        groups += [whole[start:start + 8, :] for start in range(0, depth, 8)]
    return groups


def inverse_kernel(span, pieces_ref, inverse_ref):
    inverse_factor(gram_groups(pieces_ref, span), inverse_ref)


def inverse_of(pieces, span):
    return pl.pallas_call(
        functools.partial(inverse_kernel, span),
        out_shape=jax.ShapeDtypeStruct((K, K), jnp.float32),
        in_specs=[VMEM_SPEC],
        compiler_params=pltpu.CompilerParams(vmem_limit_bytes=16 << 20),
        cost_estimate=pl.CostEstimate(
            flops=4 * K ** 3, bytes_accessed=pieces.size * 2 + 4 * K * K, transcendentals=K
        ),
    )(pieces)


def normalise_kernel(span, pieces_ref, rows_ref, inverse_ref):
    inverse_factor(gram_groups(pieces_ref, span), inverse_ref)
    for y in range(N_Y):
        rows = nt_product(pieces_ref[y, :span, :], inverse_ref[...]).astype(rows_ref.dtype)
        for x in range(N_X):
            rows_ref[x, span * y:span * (y + 1), :] = rows


def normalise(pieces, span):
    return pl.pallas_call(
        functools.partial(normalise_kernel, span),
        out_shape=(
            jax.ShapeDtypeStruct((N_X, N_Y * span, K), jnp.bfloat16),
            jax.ShapeDtypeStruct((K, K), jnp.float32),
        ),
        compiler_params=pltpu.CompilerParams(vmem_limit_bytes=16 << 20),
    )(pieces)


def parts_in(matrix, count):
    parts = []
    for _ in range(count):
        parts.append(matrix.astype(jnp.bfloat16))
        matrix = matrix - parts[-1].astype(jnp.float32)
    return parts


def products_kernel(data_ref, sketch_ref, blocks_ref):
    tokens = data_ref.shape[0]
    quarter, chunk = tokens // N_X, tokens // CHUNKS
    sketch = sketch_ref[...]
    gram = lax.dot_general(
        sketch, sketch, (((0,), (0,)), ((), ())), precision=HIGHEST,
        preferred_element_type=jnp.float32,
    )
    whole = blocks_ref.dtype == jnp.float32
    for i, part in enumerate([gram] if whole else parts_in(gram, PARTS)):
        for x in range(N_X):
            blocks_ref[x, quarter + K * i:quarter + K * (i + 1), :] = part
    both = jnp.concatenate(parts_in(sketch, 2), axis=1)
    for i in range(CHUNKS):
        product = jnp.dot(
            data_ref[chunk * i:chunk * (i + 1), :], both, preferred_element_type=jnp.float32
        )
        product = product[:, :K] + product[:, K:]
        start = chunk * i % quarter
        blocks_ref[chunk * i // quarter, start:start + chunk, :] = product.astype(blocks_ref.dtype)


def product_blocks(data, sketch, held_as):
    rows = data.shape[0] // N_X + K * (1 if held_as == jnp.float32 else PARTS)
    return pl.pallas_call(
        products_kernel,
        out_shape=jax.ShapeDtypeStruct((N_X, rows, K), held_as),
        in_specs=[VMEM_SPEC] * 2,
        compiler_params=pltpu.CompilerParams(vmem_limit_bytes=24 << 20),
    )(data, sketch)


def projection_kernel(grads_ref, rows_ref, inverse_ref, blocks_ref):
    quarter = rows_ref.shape[1]
    total = jnp.zeros((K, grads_ref.shape[1]), jnp.float32)
    for x in range(N_X):
        total = total + lax.dot_general(
            rows_ref[x], grads_ref[quarter * x:quarter * (x + 1), :], (((0,), (0,)), ((), ())),
            preferred_element_type=jnp.float32,
        )
    total = jnp.dot(
        inverse_ref[...], total, precision=HIGHEST, preferred_element_type=jnp.float32
    )
    depth = K // N_DP
    for z in range(N_Z):
        for core in range(N_CORE):
            start = (core * N_Z + z) * depth
            blocks_ref[z * N_CORE + core] = total[start:start + depth, :]


def projection_blocks(grads, rows, inverse):
    return pl.pallas_call(
        projection_kernel,
        out_shape=jax.ShapeDtypeStruct((N_DP, K // N_DP, grads.shape[1]), jnp.float32),
        in_specs=[VMEM_SPEC] * 3,
        compiler_params=pltpu.CompilerParams(vmem_limit_bytes=24 << 20),
    )(grads, rows, inverse)


def rows_product(left, right):
    return lax.dot_general(
        left, right, (((0,), (0,)), ((), ())), preferred_element_type=jnp.float32
    )


def split(matrix, count):
    parts = []
    for _ in range(count):
        high = lax.reduce_precision(matrix, 8, 7)
        parts.append(high.astype(jnp.bfloat16))
        matrix = matrix - high
    return parts


def exchange(blocks, axis, groups=None):
    return lax.all_to_all(blocks, axis, 0, 0, axis_index_groups=groups)


def scatter_sum(blocks, axis, groups=None):
    return jnp.sum(exchange(blocks, axis, groups).astype(jnp.float32), axis=0)


def gather(block, axis, count, groups=None):
    return exchange(jnp.broadcast_to(block[None], (count,) + block.shape), axis, groups)


def sum_over_tokens(partial_value):
    rows, columns = partial_value.shape
    mine = scatter_sum(partial_value.reshape(N_DP, rows // N_DP, columns), "dp")
    return gather(mine, "dp", N_DP).reshape(rows, columns)


def blocks_over_tokens(partial_value):
    rows, columns = partial_value.shape
    blocks = partial_value.reshape(N_CORE, N_Z, rows // N_DP, columns).swapaxes(0, 1)
    return blocks.reshape(N_DP, rows // N_DP, columns)


def staged_sum_over_tokens(blocks, held_as):
    mine = scatter_sum(blocks, "dp").astype(held_as)
    mine = gather(mine, "dp", N_Z, Z_GROUPS).reshape(-1, blocks.shape[2]).astype(jnp.float32)
    return lax.all_gather(mine, "dp", axis_index_groups=CORE_GROUPS, tiled=True)


def token_sums_of(data, sketch, held_as):
    tokens = data.shape[0]
    parts = 1 if held_as == jnp.float32 else PARTS
    quarter, span, depth = tokens // N_X, tokens // N_MP, K // N_Y

    def parts_of(gram):
        return [gram] if parts == 1 else split(gram, parts)

    def total(received, rows):
        received = received.astype(jnp.float32)
        pieces = received[:, rows:].reshape(received.shape[0], parts, -1, K)
        return jnp.sum(received[:, :rows], axis=0), jnp.sum(jnp.sum(pieces, axis=1), axis=0)

    blocks = product_blocks(data, sketch, held_as)
    product, gram = total(exchange(blocks, "mp", X_GROUPS), quarter)
    blocks = jnp.concatenate(
        [product.astype(held_as).reshape(N_Y, span, K)]
        + [part.reshape(N_Y, depth, K) for part in parts_of(gram)], axis=1
    )
    product, gram = total(exchange(blocks, "mp", Y_GROUPS), span)
    pieces = jnp.concatenate([product.astype(held_as)] + parts_of(gram), axis=0)
    return gather(pieces, "mp", N_Y, Y_GROUPS), span


def token_rows_of(data, sketch):
    rows, _ = normalise(*token_sums_of(data, sketch, jnp.float32))
    return exchange(rows, "mp", X_GROUPS).reshape(data.shape[0], K)


def on_device(activations, output_grads, probe_matrix):
    tokens = activations.shape[0]
    partial_value = jnp.dot(output_grads, probe_matrix, preferred_element_type=jnp.float32)
    partial_value = partial_value.astype(jnp.bfloat16)
    mine = scatter_sum(partial_value.reshape(N_MP, tokens // N_MP, K), "mp").astype(jnp.bfloat16)
    probe_rows = gather(mine, "mp", N_MP).reshape(tokens, K)

    sketch = sum_over_tokens(rows_product(activations, probe_rows))
    token_rows = token_rows_of(activations, sketch)
    partial_value = rows_product(output_grads, token_rows)
    back_sketch = staged_sum_over_tokens(blocks_over_tokens(partial_value), jnp.float32)
    unit_rows = token_rows_of(output_grads, back_sketch)
    power_sketch = sum_over_tokens(rows_product(activations, unit_rows))
    pieces, span = token_sums_of(activations, power_sketch, jnp.bfloat16)
    inverse = inverse_of(pieces, span)
    products = gather(pieces[:, :span].reshape(tokens // N_X, K), "mp", N_X, X_GROUPS)
    blocks = projection_blocks(output_grads, products, inverse)
    projection = staged_sum_over_tokens(blocks, jnp.bfloat16)
    third_basis = lax.dot_general(
        power_sketch, inverse, (((1,), (1,)), ((), ())), precision=HIGHEST,
        preferred_element_type=jnp.float32,
    )
    return (third_basis * jnp.sqrt(jnp.float32(H)), projection)


def solution(mesh):
    in_specs = (P("dp", "mp"), P("dp", "mp"), P("mp", None))
    out_specs = (P("mp", None), P(None, "mp"))
    return jax.shard_map(
        on_device, mesh=mesh, in_specs=in_specs, out_specs=out_specs, check_vma=False
    )
```

```python
import functools

import jax
import jax.numpy as jnp
from jax import lax
from jax.experimental import pallas as pl
from jax.experimental.pallas import tpu as pltpu
from jax.sharding import PartitionSpec as P

H = 8192
K = 128
N_X = 4
N_Y = 8
N_MP = N_X * N_Y
PARTS = 3
CHUNKS = 8
N_CORE = 2
N_Z = 8
N_DP = N_Z * N_CORE
X_GROUPS = [[y * N_X + x for x in range(N_X)] for y in range(N_Y)]
Y_GROUPS = [[y * N_X + x for y in range(N_Y)] for x in range(N_X)]
CORE_GROUPS = [[z * N_CORE + core for core in range(N_CORE)] for z in range(N_Z)]
Z_GROUPS = [[z * N_CORE + core for z in range(N_Z)] for core in range(N_CORE)]
HIGHEST = lax.Precision.HIGHEST
VMEM_SPEC = pl.BlockSpec(memory_space=pltpu.VMEM)


def spread(value):
    return jnp.broadcast_to(value, (8, K))


def inverse_factor(groups, inverse_ref):
    lanes = lax.broadcasted_iota(jnp.int32, (8, K), 1)
    for own in range(K // 8):
        first = 8 * own
        rows = [spread(groups[own][j:j + 1, :]) for j in range(8)]
        inner = [
            [spread(rows[i][:, first + j:first + j + 1]) for j in range(i + 1)] for i in range(8)
        ]
        factor = [[None] * 8 for _ in range(8)]
        inverse_pivots = []
        for j in range(8):
            inverse_pivots.append(1.0 / inner[j][j])
            for i in range(j + 1, 8):
                factor[i][j] = inner[i][j] * inverse_pivots[j]
            for i in range(j + 1, 8):
                for m in range(j + 1, i + 1):
                    inner[i][m] = inner[i][m] - factor[i][j] * inner[m][j]
        inside = (lanes >= first) & (lanes < first + 8)
        done = []
        for j in range(8):
            row = jnp.where(inside, jnp.where(lanes == first + j, 1.0, 0.0), rows[j])
            for m in range(j):
                row = row - factor[j][m] * done[m]
            done.append(row)
            scaled = jnp.where(lanes > first + j, 0.0, row * lax.rsqrt(inner[j][j]))
            inverse_ref[first + j:first + j + 1, :] = scaled[0:1, :]
        for g in range(own + 1, K // 8):
            kept = jnp.where(inside, 0.0, groups[g])
            columns = []
            for j in range(8):
                column = spread(groups[g][:, first + j:first + j + 1])
                for m in range(j):
                    column = column - columns[m] * factor[j][m]
                columns.append(column)
            for j in range(8):
                kept = kept - (columns[j] * inverse_pivots[j]) * done[j]
            groups[g] = kept


def nt_product(left, right):
    return lax.dot_general(
        left, right, (((1,), (1,)), ((), ())), precision=HIGHEST,
        preferred_element_type=jnp.float32,
    )


def gram_groups(pieces_ref, span):
    parts = 1 if pieces_ref.dtype == jnp.float32 else PARTS
    depth = K // N_Y
    groups = []
    for y in range(N_Y):
        whole = pieces_ref[y, span:span + depth, :].astype(jnp.float32)
        for part in range(1, parts):
            start = span + part * depth
            whole = whole + pieces_ref[y, start:start + depth, :].astype(jnp.float32)
        groups += [whole[start:start + 8, :] for start in range(0, depth, 8)]
    return groups


def inverse_kernel(span, pieces_ref, inverse_ref):
    inverse_factor(gram_groups(pieces_ref, span), inverse_ref)


def inverse_of(pieces, span):
    return pl.pallas_call(
        functools.partial(inverse_kernel, span),
        out_shape=jax.ShapeDtypeStruct((K, K), jnp.float32),
        in_specs=[VMEM_SPEC],
        compiler_params=pltpu.CompilerParams(vmem_limit_bytes=16 << 20),
        cost_estimate=pl.CostEstimate(
            flops=4 * K ** 3, bytes_accessed=pieces.size * 2 + 4 * K * K, transcendentals=K
        ),
    )(pieces)


def normalise_kernel(span, pieces_ref, rows_ref, inverse_ref):
    inverse_factor(gram_groups(pieces_ref, span), inverse_ref)
    product = jnp.concatenate([pieces_ref[y, :span, :] for y in range(N_Y)], axis=0)
    rows = nt_product(product, inverse_ref[...]).astype(rows_ref.dtype)
    for x in range(N_X):
        rows_ref[x] = rows


def normalise(pieces, span):
    return pl.pallas_call(
        functools.partial(normalise_kernel, span),
        out_shape=(
            jax.ShapeDtypeStruct((N_X, N_Y * span, K), jnp.bfloat16),
            jax.ShapeDtypeStruct((K, K), jnp.float32),
        ),
        compiler_params=pltpu.CompilerParams(vmem_limit_bytes=16 << 20),
    )(pieces)


def parts_in(matrix, count):
    parts = []
    for _ in range(count):
        parts.append(matrix.astype(jnp.bfloat16))
        matrix = matrix - parts[-1].astype(jnp.float32)
    return parts


def products_kernel(data_ref, sketch_ref, blocks_ref):
    tokens = data_ref.shape[0]
    quarter, chunk = tokens // N_X, tokens // CHUNKS
    sketch = sketch_ref[...]
    gram = lax.dot_general(
        sketch, sketch, (((0,), (0,)), ((), ())), precision=HIGHEST,
        preferred_element_type=jnp.float32,
    )
    whole = blocks_ref.dtype == jnp.float32
    for i, part in enumerate([gram] if whole else parts_in(gram, PARTS)):
        for x in range(N_X):
            blocks_ref[x, quarter + K * i:quarter + K * (i + 1), :] = part
    both = jnp.concatenate(parts_in(sketch, 2), axis=1)
    for i in range(CHUNKS):
        product = jnp.dot(
            data_ref[chunk * i:chunk * (i + 1), :], both, preferred_element_type=jnp.float32
        )
        product = product[:, :K] + product[:, K:]
        start = chunk * i % quarter
        blocks_ref[chunk * i // quarter, start:start + chunk, :] = product.astype(blocks_ref.dtype)


def product_blocks(data, sketch, held_as):
    rows = data.shape[0] // N_X + K * (1 if held_as == jnp.float32 else PARTS)
    return pl.pallas_call(
        products_kernel,
        out_shape=jax.ShapeDtypeStruct((N_X, rows, K), held_as),
        in_specs=[VMEM_SPEC] * 2,
        compiler_params=pltpu.CompilerParams(vmem_limit_bytes=24 << 20),
    )(data, sketch)


def projection_kernel(grads_ref, rows_ref, inverse_ref, blocks_ref):
    quarter = rows_ref.shape[1]
    total = jnp.zeros((K, grads_ref.shape[1]), jnp.float32)
    for x in range(N_X):
        total = total + lax.dot_general(
            rows_ref[x], grads_ref[quarter * x:quarter * (x + 1), :], (((0,), (0,)), ((), ())),
            preferred_element_type=jnp.float32,
        )
    total = jnp.dot(
        inverse_ref[...], total, precision=HIGHEST, preferred_element_type=jnp.float32
    )
    depth = K // N_DP
    for z in range(N_Z):
        for core in range(N_CORE):
            start = (core * N_Z + z) * depth
            blocks_ref[z * N_CORE + core] = total[start:start + depth, :]


def projection_blocks(grads, rows, inverse):
    return pl.pallas_call(
        projection_kernel,
        out_shape=jax.ShapeDtypeStruct((N_DP, K // N_DP, grads.shape[1]), jnp.float32),
        in_specs=[VMEM_SPEC] * 3,
        compiler_params=pltpu.CompilerParams(vmem_limit_bytes=24 << 20),
    )(grads, rows, inverse)


def rows_product(left, right):
    return lax.dot_general(
        left, right, (((0,), (0,)), ((), ())), preferred_element_type=jnp.float32
    )


def split(matrix, count):
    parts = []
    for _ in range(count):
        high = lax.reduce_precision(matrix, 8, 7)
        parts.append(high.astype(jnp.bfloat16))
        matrix = matrix - high
    return parts


def exchange(blocks, axis, groups=None):
    return lax.all_to_all(blocks, axis, 0, 0, axis_index_groups=groups)


def scatter_sum(blocks, axis, groups=None):
    return jnp.sum(exchange(blocks, axis, groups).astype(jnp.float32), axis=0)


def gather(block, axis, count, groups=None):
    return exchange(jnp.broadcast_to(block[None], (count,) + block.shape), axis, groups)


def sum_over_tokens(partial_value):
    rows, columns = partial_value.shape
    mine = scatter_sum(partial_value.reshape(N_DP, rows // N_DP, columns), "dp")
    return gather(mine, "dp", N_DP).reshape(rows, columns)


def blocks_over_tokens(partial_value):
    rows, columns = partial_value.shape
    blocks = partial_value.reshape(N_CORE, N_Z, rows // N_DP, columns).swapaxes(0, 1)
    return blocks.reshape(N_DP, rows // N_DP, columns)


def staged_sum_over_tokens(blocks, held_as):
    mine = scatter_sum(blocks, "dp").astype(held_as)
    mine = gather(mine, "dp", N_Z, Z_GROUPS).reshape(-1, blocks.shape[2]).astype(jnp.float32)
    return lax.all_gather(mine, "dp", axis_index_groups=CORE_GROUPS, tiled=True)


def token_sums_of(data, sketch, held_as):
    tokens = data.shape[0]
    parts = 1 if held_as == jnp.float32 else PARTS
    quarter, span, depth = tokens // N_X, tokens // N_MP, K // N_Y

    def parts_of(gram):
        return [gram] if parts == 1 else split(gram, parts)

    def total(received, rows):
        received = received.astype(jnp.float32)
        pieces = received[:, rows:].reshape(received.shape[0], parts, -1, K)
        return jnp.sum(received[:, :rows], axis=0), jnp.sum(jnp.sum(pieces, axis=1), axis=0)

    blocks = product_blocks(data, sketch, held_as)
    product, gram = total(exchange(blocks, "mp", X_GROUPS), quarter)
    blocks = jnp.concatenate(
        [product.astype(held_as).reshape(N_Y, span, K)]
        + [part.reshape(N_Y, depth, K) for part in parts_of(gram)], axis=1
    )
    product, gram = total(exchange(blocks, "mp", Y_GROUPS), span)
    pieces = jnp.concatenate([product.astype(held_as)] + parts_of(gram), axis=0)
    return gather(pieces, "mp", N_Y, Y_GROUPS), span


def token_rows_of(data, sketch):
    rows, _ = normalise(*token_sums_of(data, sketch, jnp.float32))
    return exchange(rows, "mp", X_GROUPS).reshape(data.shape[0], K)


def on_device(activations, output_grads, probe_matrix):
    tokens = activations.shape[0]
    partial_value = jnp.dot(output_grads, probe_matrix, preferred_element_type=jnp.float32)
    partial_value = partial_value.astype(jnp.bfloat16)
    mine = scatter_sum(partial_value.reshape(N_MP, tokens // N_MP, K), "mp").astype(jnp.bfloat16)
    probe_rows = gather(mine, "mp", N_MP).reshape(tokens, K)

    sketch = sum_over_tokens(rows_product(activations, probe_rows))
    token_rows = token_rows_of(activations, sketch)
    partial_value = rows_product(output_grads, token_rows)
    back_sketch = staged_sum_over_tokens(blocks_over_tokens(partial_value), jnp.float32)
    unit_rows = token_rows_of(output_grads, back_sketch)
    power_sketch = sum_over_tokens(rows_product(activations, unit_rows))
    pieces, span = token_sums_of(activations, power_sketch, jnp.bfloat16)
    inverse = inverse_of(pieces, span)
    products = gather(pieces[:, :span].reshape(tokens // N_X, K), "mp", N_X, X_GROUPS)
    blocks = projection_blocks(output_grads, products, inverse)
    projection = staged_sum_over_tokens(blocks, jnp.bfloat16)
    third_basis = lax.dot_general(
        power_sketch, inverse, (((1,), (1,)), ((), ())), precision=HIGHEST,
        preferred_element_type=jnp.float32,
    )
    return (third_basis * jnp.sqrt(jnp.float32(H)), projection)


def solution(mesh):
    in_specs = (P("dp", "mp"), P("dp", "mp"), P("mp", None))
    out_specs = (P("mp", None), P(None, "mp"))
    return jax.shard_map(
        on_device, mesh=mesh, in_specs=in_specs, out_specs=out_specs, check_vma=False
    )
```
